512 devices in a mesh: row: 64 (over y_hi, x, z), col: 8 (over y_lo, core).
Axes of the slice: x: 4, y: 8 (y_hi: 2, y_lo: 4; y = y_hi * 4 + y_lo), z: 8, core: 2. Of those that a mesh axis runs over, the one named last changes fastest.
Arguments:
- features: bfloat16 [65536, 1024], P(('row', 'col')), may hold values from -6 to 6
- history: bfloat16 [65536, 1024], P(('row', 'col')), may hold values from -6 to 6
- degree: int32 [65536], P(('row', 'col')), may hold values from 8 to 64
- adj_tiles: bfloat16 [3072, 128, 128], P(('row', 'col')), may hold values from 0 to 3, as said below
- tile_index: int32 [3072], P(('row', 'col')), may hold values from 0 to 23, as said below
- tile_count: int32 [512], P(('row', 'col')), may hold values from 3 to 6, as said below
- weight: bfloat16 [1024, 1024], P(None, 'col'), may hold values from -0.1875 to 0.1875
- cotangent: bfloat16 [65536, 1024], P(('row', 'col')), may hold values from -6 to 6
Outputs:
- layer_out: bfloat16 [65536, 1024], P(('row', 'col'))
- grad_features: bfloat16 [65536, 1024], P(('row', 'col'))
- grad_weight: float32 [1024, 1024], P(None, 'col')
The draws below stay inside these ranges and needn't reach their ends.
Inputs may be any that keep to these rules, and one draw needn't show every extreme that they name: `adj_tiles`: whole numbers: the edge counts of a tile's entries. Slots from tile_count on of a device are never read. `tile_index`: the codes of one device's 6 slots are distinct. Its first three slots hold tiles whose column block lies in the first, the last and the middle third of the 3 m column blocks, in that order. `tile_count`: some device has 6 live slots in every draw.
All inputs are finite; a program needn't handle non-finite values.
Results may differ from the reference program's by a relative error of at most 0.014.
Values may be sent and summed in bfloat16 or wider, within the bound.
No kernel may reach another device: no remote copies, remote signals or barrier semaphores. Data moves between devices by JAX's collectives and lax.ppermute only.
A program may use at most 64 MiB of HBM per device.

```python
import math
import jax
import jax.numpy as jnp
from jax import lax

D = 1024
TILE = 128
SLAB = 128
PART = 1024
NODES = 65536
MAXT = 6
N_ROW = 64
N_COL = 8


def tile_layout(key):
    inner_key = jax.random.fold_in(key, 7)
    devices_all = N_ROW * N_COL
    blocks = SLAB // TILE
    src_width = 3 * blocks
    dest_blocks = blocks * N_COL
    positions = 3 * blocks * blocks * N_COL
    score_key, count_key, pick_key, dest_key, src_key = jax.random.split(inner_key, 5)
    dests = jax.random.randint(dest_key, (devices_all, 3), 0, dest_blocks)
    offsets = jax.random.randint(src_key, (devices_all, 3), 0, blocks)
    thirds = jnp.array([0, 2, 1], dtype=jnp.int32)[None, :]
    forced = (dests * src_width + thirds * blocks + offsets).astype(jnp.int32)
    scores = jax.random.randint(score_key, (devices_all, positions), 0, 2 ** 19) * positions + jnp.arange(positions, dtype=jnp.int32)[None, :]
    codes_all = jnp.arange(positions, dtype=jnp.int32)[None, :]
    for which in range(3):
        scores = jnp.where(codes_all == forced[:, which:which + 1], which - 3, scores)
    ranked = jnp.argsort(scores, axis=1)
    slot_codes = ranked[:, :MAXT].astype(jnp.int32)
    live_counts = jax.random.randint(count_key, (devices_all,), 3, MAXT + 1)
    busiest = jax.random.randint(pick_key, (), 0, devices_all)
    live_counts = jnp.where(jnp.arange(devices_all) == busiest, MAXT, live_counts).astype(jnp.int32)
    return (slot_codes.reshape(-1), live_counts)


def draw_tile_index(key, part):
    return tile_layout(key)[0]


def draw_tile_count(key, part):
    return tile_layout(key)[1]


def draw_adj_tiles(key, part):
    mask_key, value_key = jax.random.split(jax.random.fold_in(key, 11))
    shape_all = (MAXT * N_ROW * N_COL, TILE, TILE)
    present = (jax.random.randint(mask_key, shape_all, 0, TILE) < 4).astype(jnp.int32)
    counted = jax.random.randint(value_key, shape_all, 1, 4)
    return (present * counted).astype(jnp.bfloat16)


def set_ends(entries, rng, low, high):
    spot = [jax.random.randint(jax.random.fold_in(rng, axis), (), 0, length) for axis, length in enumerate(entries.shape)]
    longest = entries.shape.index(max(entries.shape))
    beside = spot[:longest] + [(spot[longest] + 1) % entries.shape[longest]] + spot[longest + 1:]
    return entries.at[tuple(spot)].set(low).at[tuple(beside)].set(high)


def block_levels(rng, shape, cuts, smallest, largest):
    loudness, own = 1.0, jax.random.fold_in(rng, 6)
    for axis_at, shards_of in cuts:
        draws = jnp.exp(jax.random.uniform(jax.random.fold_in(own, axis_at), (shards_of,), jnp.float32, smallest / len(cuts), largest / len(cuts)))
        loudness = loudness * jnp.repeat(draws, shape[axis_at] // shards_of).reshape([-1 if axis == axis_at else 1 for axis in range(len(shape))])
    return loudness


def noise(own_key, dims, scale, bound, shards=(), kind=jnp.bfloat16):
    result = jax.random.normal(own_key, dims, jnp.float32) * scale
    if len(shards) > 0:
        result = block_levels(own_key, dims, shards, -0.22, 0.18) * result
    return jnp.clip(result, min=-bound, max=bound).astype(kind)


def setup_inputs(seed: int = 0) -> dict:
    seeds = jax.random.split(jax.random.key(seed), 9)
    return {
        "features": noise(seeds[0], (NODES, D), 1.0, 6.0, ((0, 512),)),
        "history": noise(seeds[1], (NODES, D), 1.0, 6.0, ((0, 512),)),
        "degree": set_ends(jax.random.randint(seeds[2], (NODES,), 8, 65), jax.random.fold_in(seeds[2], 1), 8, 64).astype(jnp.int32),
        "adj_tiles": draw_adj_tiles(jax.random.fold_in(seeds[8], 71), 0),
        "tile_index": draw_tile_index(jax.random.fold_in(seeds[8], 71), 0),
        "tile_count": draw_tile_count(jax.random.fold_in(seeds[8], 71), 0),
        "weight": noise(seeds[6], (D, D), D ** -0.5, 0.1875, ((1, 8),)),
        "cotangent": noise(seeds[7], (NODES, D), 1.0, 6.0, ((0, 512),)),
    }


def inverse_root(degree):
    return 1.0 / jnp.sqrt(degree.astype(jnp.float32))

def silu_slope(pre_act):
    sigmoid = jax.nn.sigmoid(pre_act)
    return sigmoid * (1.0 + pre_act * (1.0 - sigmoid))

def dense_block(tile_stack, slot_codes, live_tiles):
    blocks = SLAB // TILE
    positions = 3 * blocks * blocks * N_COL
    used = (jnp.arange(tile_stack.shape[0], dtype=jnp.int32) < live_tiles).astype(jnp.float32)
    onehot = (slot_codes[:, None] == jnp.arange(positions, dtype=jnp.int32)[None, :]).astype(jnp.float32) * used[:, None]
    placed = jnp.einsum('tk,tab->kab', onehot, tile_stack.astype(jnp.float32), precision=lax.Precision.HIGHEST)
    placed = placed.reshape(blocks * N_COL, 3 * blocks, TILE, TILE).transpose(0, 2, 1, 3)
    return placed.reshape(PART, 3 * SLAB).astype(jnp.bfloat16)

def reference(features, history, degree, adj_tiles, tile_index, tile_count, weight, cotangent):
    scale_all = inverse_root(degree)
    own_src = (features.astype(jnp.float32) * scale_all[:, None]).astype(jnp.bfloat16).reshape(N_ROW, N_COL, SLAB, D)
    hist_src = (history.astype(jnp.float32) * scale_all[:, None]).astype(jnp.bfloat16).reshape(N_ROW, N_COL, SLAB, D)
    hist_pad = jnp.pad(hist_src, ((1, 1), (0, 0), (0, 0), (0, 0)))
    tiles_by = adj_tiles.reshape(N_ROW, N_COL, MAXT, TILE, TILE)
    codes_by = tile_index.reshape(N_ROW, N_COL, MAXT)
    live_by = tile_count.reshape(N_ROW, N_COL)
    scale_by = scale_all.reshape(N_ROW, PART)
    cot_by = cotangent.reshape(N_ROW, PART, D)

    def partition(grad_acc, row_at):
        before = hist_pad[row_at]
        after = hist_pad[row_at + 2]
        sources = jnp.concatenate([before, own_src[row_at], after], axis=1)
        blocks_dense = jax.vmap(dense_block)(tiles_by[row_at], codes_by[row_at], live_by[row_at])

        def col_partial(pair):
            block_mat, source_rows = pair
            return jnp.dot(block_mat, source_rows, preferred_element_type=jnp.float32).astype(jnp.bfloat16)
        partials = lax.map(col_partial, (blocks_dense, sources))
        raw_sum = lax.optimization_barrier(jnp.sum(partials.astype(jnp.float32), axis=0))
        row_scale = scale_by[row_at]
        aggregated = (raw_sum * row_scale[:, None]).astype(jnp.bfloat16)
        pre_act = jnp.dot(aggregated, weight, preferred_element_type=jnp.float32)
        layer_out = jax.nn.silu(pre_act).astype(jnp.bfloat16)
        grad_pre = (cot_by[row_at].astype(jnp.float32) * silu_slope(pre_act)).astype(jnp.bfloat16)
        back_prop = lax.dot_general(grad_pre, weight, (((1,), (1,)), ((), ())), preferred_element_type=jnp.float32)
        dest_grad = (back_prop * row_scale[:, None]).astype(jnp.bfloat16)
        middles = blocks_dense[:, :, SLAB:2 * SLAB]
        grad_src = jnp.einsum('cps,pd->csd', middles.astype(jnp.float32), dest_grad.astype(jnp.float32), precision=lax.Precision.HIGHEST)
        grad_nodes = (grad_src.reshape(PART, D) * row_scale[:, None]).astype(jnp.bfloat16)
        weight_term = lax.dot_general(aggregated, grad_pre, (((0,), (0,)), ((), ())), preferred_element_type=jnp.float32)
        return (grad_acc + weight_term, (layer_out, grad_nodes))
    grad_acc, (outputs, grads) = lax.scan(partition, jnp.zeros((D, D), jnp.float32), jnp.arange(N_ROW, dtype=jnp.int32))
    grad_weight = grad_acc * (1.0 / math.sqrt(NODES))
    return (outputs.reshape(NODES, D), grads.reshape(NODES, D), grad_weight)
```

```python
import functools
import math

import jax
import jax.numpy as jnp
from jax import lax
from jax.experimental import pallas as pl
from jax.experimental.pallas import tpu as pltpu
from jax.sharding import PartitionSpec as P

TILE = 128
F32 = jnp.float32
BF16 = jnp.bfloat16


def neighbours(x, axis):
    count = lax.axis_size(axis)
    up = [(i, i + 1) for i in range(count - 1)]
    down = [(i + 1, i) for i in range(count - 1)]
    return lax.ppermute(x, axis, up), lax.ppermute(x, axis, down)


def inverse_root(degree):
    return 1.0 / jnp.sqrt(degree.astype(F32))


def vmem(count):
    return [pl.BlockSpec(memory_space=pltpu.VMEM)] * count


def smem(count):
    return [pl.BlockSpec(memory_space=pltpu.SMEM)] * count


def aggregate_kernel(index, count, tiles, before, own, after, partial, middle, block):
    slots, slab = tiles.shape[0], own.shape[0]
    width = 3 * slab // TILE
    block[...] = jnp.zeros_like(block)
    for slot in range(slots):

        @pl.when(slot < count[0])
        def _():
            code = index[slot]
            row = pl.multiple_of((code // width) * TILE, TILE)
            col = pl.multiple_of((code % width) * TILE, TILE)
            block[pl.ds(row, TILE), pl.ds(col, TILE)] = tiles[slot]

    middle[...] = block[:, slab : 2 * slab]
    part_rows = partial.shape[0]
    step = 256

    def rows(at, carry):
        here = pl.ds(pl.multiple_of(at * step, step), step)
        total = jnp.dot(block[here, :slab], before[...], preferred_element_type=F32)
        total += jnp.dot(block[here, slab : 2 * slab], own[...], preferred_element_type=F32)
        total += jnp.dot(block[here, 2 * slab :], after[...], preferred_element_type=F32)
        partial[here, :] = total.astype(BF16)
        return carry

    lax.fori_loop(0, part_rows // step, rows, 0)


def aggregate(index, count, tiles, before, own, after, part_rows):
    slab, width = own.shape
    flops = 2 * part_rows * 3 * slab * width
    return pl.pallas_call(
        aggregate_kernel,
        name="aggregate",
        out_shape=(
            jax.ShapeDtypeStruct((part_rows, width), BF16),
            jax.ShapeDtypeStruct((part_rows, slab), BF16),
        ),
        in_specs=smem(2) + vmem(4),
        out_specs=tuple(vmem(2)),
        scratch_shapes=[pltpu.VMEM((part_rows, 3 * slab), BF16)],
        cost_estimate=pl.CostEstimate(flops=flops, bytes_accessed=4 << 20, transcendentals=0),
    )(index, count, tiles, before, own, after)


def layer_kernel(agg, scale, weight, cot, out, grad):
    rows, width = agg.shape
    step = 256
    scaled = (agg[...].astype(F32) * scale[...]).astype(BF16)

    for at in range(0, width, step):
        here = slice(at, at + step)
        pre = jnp.dot(scaled, weight[:, here], preferred_element_type=F32)
        sig = jax.nn.sigmoid(pre)
        out[:, here] = (pre * sig).astype(BF16)
        slope = sig * (1.0 + pre * (1.0 - sig))
        grad[:, here] = (cot[:, here].astype(F32) * slope * scale[...]).astype(BF16)


def layer(agg, scale, weight, cot):
    rows, width = agg.shape
    return pl.pallas_call(
        layer_kernel,
        name="layer",
        out_shape=(jax.ShapeDtypeStruct((rows, width), BF16),) * 2,
        in_specs=vmem(4),
        out_specs=tuple(vmem(2)),
        cost_estimate=pl.CostEstimate(
            flops=2 * rows * width * width, bytes_accessed=3 << 20, transcendentals=rows * width
        ),
    )(agg, scale, weight, cot)


def sources_kernel(grads, middle, weight, scale, out):
    mixed = lax.dot_general(
        middle[...], grads[...], (((0,), (0,)), ((), ())), preferred_element_type=F32
    ).astype(BF16)
    back = lax.dot_general(
        mixed, weight[...], (((1,), (1,)), ((), ())), preferred_element_type=F32
    )
    out[...] = (back * scale[...]).astype(BF16)


def source_grads(grads, middle, weight, scale):
    slab, width = middle.shape[1], grads.shape[1]
    return pl.pallas_call(
        sources_kernel,
        name="source_grads",
        out_shape=jax.ShapeDtypeStruct((slab, width), BF16),
        in_specs=vmem(4),
        out_specs=pl.BlockSpec(memory_space=pltpu.VMEM),
        cost_estimate=pl.CostEstimate(
            flops=4 * slab * width * width, bytes_accessed=5 << 20, transcendentals=0
        ),
    )(grads, middle, weight, scale)


def per_device(features, history, degree, adj_tiles, tile_index, tile_count, weight, cotangent):
    slab, width = features.shape
    cols, rows = lax.axis_size("col"), lax.axis_size("row")
    part_rows = slab * cols
    scale = inverse_root(degree)[:, None]
    hist_src = (history.astype(F32) * scale).astype(BF16)
    before, after = neighbours(hist_src, "row")
    own_src = (features.astype(F32) * scale).astype(BF16)
    whole_weight = lax.all_gather(weight, "col", axis=1, tiled=True)
    partial, middle = aggregate(
        tile_index, tile_count, adj_tiles, before, own_src, after, part_rows
    )
    agg = lax.psum_scatter(partial, "col", scatter_dimension=0, tiled=True)
    layer_out, grad = layer(agg, scale, whole_weight, cotangent)
    all_grad = lax.all_gather(grad, "col", axis=0, tiled=True)
    agg_cols = lax.all_to_all(agg, "col", 1, 0, tiled=True)
    term = lax.dot_general(
        agg_cols, all_grad, (((0,), (0,)), ((), ())), preferred_element_type=F32
    )
    chunk = width // cols // rows
    pieces = lax.all_to_all(
        term.astype(BF16).reshape(rows, chunk, width), "row", 0, 0, tiled=True
    )
    total = jnp.sum(pieces.astype(F32), axis=0) * (1.0 / math.sqrt(part_rows * rows))
    owned = lax.all_to_all(total, "col", 1, 0, tiled=True)
    owned = owned.reshape(cols, chunk, width // cols)
    every = lax.all_gather(owned, "row", axis=0)
    grad_weight = every.transpose(1, 0, 2, 3).reshape(width, width // cols)
    grad_features = source_grads(all_grad, middle, whole_weight, scale)
    return layer_out, grad_features, grad_weight


def solution(mesh):
    both = ("row", "col")
    in_specs = (
        P(both, None),
        P(both, None),
        P(both),
        P(both, None, None),
        P(both),
        P(both),
        P(None, "col"),
        P(both, None),
    )
    out_specs = (P(both, None), P(both, None), P(None, "col"))
    return jax.shard_map(
        per_device, mesh=mesh, in_specs=in_specs, out_specs=out_specs, check_vma=False
    )
```

```python
import math

import jax
import jax.numpy as jnp
from jax import lax
from jax.experimental import pallas as pl
from jax.experimental.pallas import tpu as pltpu
from jax.sharding import PartitionSpec as P

TILE = 128
CORES = 2
RING = 8
F32 = jnp.float32
BF16 = jnp.bfloat16


def neighbours(x, axis):
    count = lax.axis_size(axis)
    up = [(i, i + 1) for i in range(count - 1)]
    down = [(i + 1, i) for i in range(count - 1)]
    return lax.ppermute(x, axis, up), lax.ppermute(x, axis, down)


def inverse_root(degree):
    return 1.0 / jnp.sqrt(degree.astype(F32))


def swap(x):
    return lax.ppermute(x, "col", [(i, i ^ 1) for i in range(lax.axis_size("col"))])


def rotate(x, by):
    cols = lax.axis_size("col")
    chips = cols // CORES
    pairs = [(i, (i // CORES + by) % chips * CORES + i % CORES) for i in range(cols)]
    return lax.ppermute(x, "col", pairs)


def gather(x):
    chips = lax.axis_size("col") // CORES
    same = [x] + [rotate(x, by) for by in range(1, chips)]
    return same + [swap(block) for block in same]


def origins(me, chips):
    chip, core = me // CORES, me % CORES
    same = [(chip - by + chips) % chips * CORES + core for by in range(chips)]
    return same + [at + 1 - 2 * core for at in same]


def vmem(count):
    return [pl.BlockSpec(memory_space=pltpu.VMEM)] * count


def smem(count):
    return [pl.BlockSpec(memory_space=pltpu.SMEM)] * count


def aggregate_kernel(
    where, index, count, tiles, before, feats, after, scale, mine, theirs, middle, block
):
    slots, slab = tiles.shape[0], feats.shape[0]
    width = 3 * slab // TILE
    half = mine.shape[0]
    chips = half // slab
    chip, core = where[0] // CORES, where[0] % CORES
    block[...] = jnp.zeros_like(block)
    middle[...] = jnp.zeros_like(middle)
    for slot in range(slots):

        @pl.when(slot < count[0])
        def _():
            code = index[slot]
            dest, src = code // width, code % width
            other = (dest % CORES + core) % CORES * chips
            ahead = (dest // CORES - chip + chips) % chips
            behind = (chip - dest // CORES + chips) % chips
            row = pl.multiple_of((other + ahead) * TILE, TILE)
            col = pl.multiple_of(src * TILE, TILE)
            block[pl.ds(row, TILE), pl.ds(col, TILE)] = tiles[slot]

            @pl.when(src == 1)
            def _():
                at = pl.multiple_of((other + behind) * TILE, TILE)
                middle[pl.ds(at, TILE), :] = tiles[slot]

    own = (feats[...].astype(F32) * scale[...]).astype(BF16)
    step = 256
    for out, base in ((theirs, half), (mine, 0)):

        def rows(at, carry, out=out, base=base):
            here = pl.ds(pl.multiple_of(base + at * step, step), step)
            total = jnp.dot(block[here, :slab], before[...], preferred_element_type=F32)
            total += jnp.dot(block[here, slab : 2 * slab], own, preferred_element_type=F32)
            total += jnp.dot(block[here, 2 * slab :], after[...], preferred_element_type=F32)
            out[pl.ds(pl.multiple_of(at * step, step), step), :] = total.astype(BF16)
            return carry

        lax.fori_loop(0, half // step, rows, 0)


def aggregate(where, index, count, tiles, before, feats, after, scale, part_rows):
    slab, width = feats.shape
    flops = 2 * part_rows * 3 * slab * width
    return pl.pallas_call(
        aggregate_kernel,
        name="aggregate",
        out_shape=(
            jax.ShapeDtypeStruct((part_rows // 2, width), BF16),
            jax.ShapeDtypeStruct((part_rows // 2, width), BF16),
            jax.ShapeDtypeStruct((part_rows, slab), BF16),
        ),
        in_specs=smem(3) + vmem(5),
        out_specs=tuple(vmem(3)),
        scratch_shapes=[pltpu.VMEM((part_rows, 3 * slab), BF16)],
        cost_estimate=pl.CostEstimate(flops=flops, bytes_accessed=4 << 20, transcendentals=0),
    )(where, index, count, tiles, before, feats, after, scale)


def assemble_kernel(where, *refs):
    *blocks, out = refs
    cols = blocks[0].shape[1]
    for at, block in zip(origins(where[0], len(blocks) // CORES), blocks):
        out[:, pl.ds(pl.multiple_of(at * cols, cols), cols)] = block[...]


def assemble(where, blocks):
    depth, cols = blocks[0].shape
    width = cols * len(blocks)
    return pl.pallas_call(
        assemble_kernel,
        name="assemble",
        out_shape=jax.ShapeDtypeStruct((depth, width), BF16),
        in_specs=smem(1) + vmem(len(blocks)),
        out_specs=pl.BlockSpec(memory_space=pltpu.VMEM),
        cost_estimate=pl.CostEstimate(flops=0, bytes_accessed=4 << 20, transcendentals=0),
    )(where, *blocks)


def layer_kernel(mine, other, one, two, three, scale, weight, cot, out, grad, pieces):
    slab, width = one.shape
    cols = pieces.shape[2]
    total = mine[...].astype(F32) + other[...].astype(F32)
    total += one[...].astype(F32) + two[...].astype(F32) + three[...].astype(F32)
    kept = total.astype(BF16)
    for at in range(width // cols):
        pieces[at] = kept[:, at * cols : (at + 1) * cols]
    scaled = (total * scale[...]).astype(BF16)
    step = 256
    for at in range(0, width, step):
        here = slice(at, at + step)
        pre = jnp.dot(scaled, weight[:, here], preferred_element_type=F32)
        sig = jax.nn.sigmoid(pre)
        out[:, here] = (pre * sig).astype(BF16)
        slope = sig * (1.0 + pre * (1.0 - sig))
        grad[:, here] = (cot[:, here].astype(F32) * slope * scale[...]).astype(BF16)


def layer(mine, other, arrived, scale, weight, cot):
    slab, width = cot.shape
    cols = TILE
    whole = lambda *shape: pl.BlockSpec(shape, lambda i: (0,) * len(shape))
    row = whole(slab, width)
    return pl.pallas_call(
        layer_kernel,
        name="layer",
        grid=(1,),
        out_shape=(
            jax.ShapeDtypeStruct((slab, width), BF16),
            jax.ShapeDtypeStruct((slab, width), BF16),
            jax.ShapeDtypeStruct((width // cols, slab, cols), BF16),
        ),
        in_specs=[row] * 5 + [whole(slab, 1), whole(width, width), row],
        out_specs=(row, row, whole(width // cols, slab, cols)),
        cost_estimate=pl.CostEstimate(
            flops=2 * slab * width * width, bytes_accessed=4 << 20, transcendentals=slab * width
        ),
    )(mine, other, *arrived, scale, weight, cot)


def term_kernel(where, aggs, *refs):
    *grads, out = refs
    blocks, _, rows, cols = out.shape
    total = None
    for at, grad in zip(origins(where[0], len(grads) // CORES), grads):
        part = lax.dot_general(
            aggs[at], grad[...], (((0,), (0,)), ((), ())), preferred_element_type=F32
        )
        total = part if total is None else total + part
    total = total.astype(BF16)
    for i in range(blocks):
        for j in range(out.shape[1]):
            out[i, j] = total[i * rows : (i + 1) * rows, j * cols : (j + 1) * cols]


def term(where, aggs, grads):
    blocks, slab, cols = aggs.shape
    width = grads[0].shape[1]
    return pl.pallas_call(
        term_kernel,
        name="term",
        out_shape=jax.ShapeDtypeStruct((RING, width // cols, cols // RING, cols), BF16),
        in_specs=smem(1) + vmem(1 + len(grads)),
        out_specs=pl.BlockSpec(memory_space=pltpu.VMEM),
        cost_estimate=pl.CostEstimate(
            flops=2 * slab * width * width, bytes_accessed=3 << 20, transcendentals=0
        ),
    )(where, aggs, *grads)


def sources_kernel(middle, weight, scale, *refs):
    *grads, out = refs
    slab = grads[0].shape[0]
    mixed = None
    for at, grad in enumerate(grads):
        part = lax.dot_general(
            middle[at * slab : (at + 1) * slab, :],
            grad[...],
            (((0,), (0,)), ((), ())),
            preferred_element_type=F32,
        )
        mixed = part if mixed is None else mixed + part
    back = lax.dot_general(
        mixed.astype(BF16), weight[...], (((1,), (1,)), ((), ())), preferred_element_type=F32
    )
    out[...] = (back * scale[...]).astype(BF16)


def source_grads(middle, weight, scale, grads):
    slab, width = grads[0].shape
    return pl.pallas_call(
        sources_kernel,
        name="source_grads",
        out_shape=jax.ShapeDtypeStruct((slab, width), BF16),
        in_specs=vmem(3 + len(grads)),
        out_specs=pl.BlockSpec(memory_space=pltpu.VMEM),
        cost_estimate=pl.CostEstimate(
            flops=4 * slab * width * width, bytes_accessed=5 << 20, transcendentals=0
        ),
    )(middle, weight, scale, *grads)


def per_device(features, history, degree, adj_tiles, tile_index, tile_count, weight, cotangent):
    slab, width = features.shape
    cols, rows = lax.axis_size("col"), lax.axis_size("row")
    chips = cols // CORES
    part_rows = slab * cols
    outer = rows // RING
    near = [[RING * i + j for j in range(RING)] for i in range(outer)]
    far = [[RING * i + j for i in range(outer)] for j in range(RING)]
    where = lax.axis_index("col").astype(jnp.int32)[None]
    scale = inverse_root(degree)[:, None]
    hist_src = (history.astype(F32) * scale).astype(BF16)
    before, after = neighbours(hist_src, "row")
    weights = gather(weight)
    mine, theirs, middle = aggregate(
        where, tile_index, tile_count, adj_tiles, before, features, after, scale, part_rows
    )
    other = swap(theirs)
    arrived = []
    for by in range(1, chips):
        here = slice(by * slab, (by + 1) * slab)
        pair = mine[here].astype(F32) + other[here].astype(F32)
        arrived.append(rotate(pair.astype(BF16), by))
    whole_weight = assemble(where, weights)
    layer_out, grad, pieces = layer(mine, other, arrived, scale, whole_weight, cotangent)
    grads = gather(grad)
    aggs = lax.all_to_all(pieces, "col", 0, 0, tiled=True)
    parts = term(where, aggs, grads)
    grad_features = source_grads(middle, whole_weight, scale, grads)

    def total(x):
        return jnp.sum(x.astype(F32), axis=0)

    def spread(x, groups):
        count = len(groups[0])
        every = jnp.broadcast_to(x[None], (count, *x.shape))
        return lax.all_to_all(every, "row", 0, 0, tiled=True, axis_index_groups=groups)

    summed = lax.all_to_all(parts, "row", 0, 0, tiled=True, axis_index_groups=near)
    owned = lax.all_to_all(total(summed).astype(BF16), "col", 0, 0, tiled=True)
    done = total(spread(owned, far)) * (1.0 / math.sqrt(part_rows * rows))
    every = spread(done.astype(BF16), near)
    grad_weight = every.astype(F32).transpose(1, 0, 2, 3).reshape(width, width // cols)
    return layer_out, grad_features, grad_weight


def solution(mesh):
    both = ("row", "col")
    in_specs = (
        P(both, None),
        P(both, None),
        P(both),
        P(both, None, None),
        P(both),
        P(both),
        P(None, "col"),
        P(both, None),
    )
    out_specs = (P(both, None), P(both, None), P(None, "col"))
    return jax.shard_map(
        per_device, mesh=mesh, in_specs=in_specs, out_specs=out_specs, check_vma=False
    )
```

```python
import math

import jax
import jax.numpy as jnp
from jax import lax
from jax.experimental import pallas as pl
from jax.experimental.pallas import tpu as pltpu
from jax.sharding import PartitionSpec as P

TILE = 128
CORES = 2
RING = 8
GRANT = 16 << 20
F32 = jnp.float32
BF16 = jnp.bfloat16


def neighbours(x, axis):
    count = lax.axis_size(axis)
    up = [(i, i + 1) for i in range(count - 1)]
    down = [(i + 1, i) for i in range(count - 1)]
    return lax.ppermute(x, axis, up), lax.ppermute(x, axis, down)


def inverse_root(degree):
    return 1.0 / jnp.sqrt(degree.astype(F32))


def swap(x):
    return lax.ppermute(x, "col", [(i, i ^ 1) for i in range(lax.axis_size("col"))])


def rotate(x, by):
    cols = lax.axis_size("col")
    chips = cols // CORES
    pairs = [(i, (i // CORES + by) % chips * CORES + i % CORES) for i in range(cols)]
    return lax.ppermute(x, "col", pairs)


def gather(x):
    chips = lax.axis_size("col") // CORES
    same = [x] + [rotate(x, by) for by in range(1, chips)]
    return same + [swap(block) for block in same]


def origins(me, chips):
    chip, core = me // CORES, me % CORES
    same = [(chip - by + chips) % chips * CORES + core for by in range(chips)]
    return same + [at + 1 - 2 * core for at in same]


def vmem(count):
    return [pl.BlockSpec(memory_space=pltpu.VMEM)] * count


def smem(count):
    return [pl.BlockSpec(memory_space=pltpu.SMEM)] * count


def aggregate_kernel(
    where, index, count, tiles, before, feats, after, scale, mine, theirs, middle, block
):
    slots, slab = tiles.shape[0], feats.shape[0]
    width = 3 * slab // TILE
    half = mine.shape[0]
    chips = half // slab
    chip, core = where[0] // CORES, where[0] % CORES
    block[...] = jnp.zeros_like(block)
    middle[...] = jnp.zeros_like(middle)
    for slot in range(slots):

        @pl.when(slot < count[0])
        def _():
            code = index[slot]
            dest, src = code // width, code % width
            other = (dest % CORES + core) % CORES * chips
            ahead = (dest // CORES - chip + chips) % chips
            behind = (chip - dest // CORES + chips) % chips
            row = pl.multiple_of((other + ahead) * TILE, TILE)
            col = pl.multiple_of(src * TILE, TILE)
            block[pl.ds(row, TILE), pl.ds(col, TILE)] = tiles[slot]

            @pl.when(src == 1)
            def _():
                at = pl.multiple_of((other + behind) * TILE, TILE)
                middle[pl.ds(at, TILE), :] = tiles[slot]

    own = (feats[...].astype(F32) * scale[...]).astype(BF16)
    step = 256
    for out, base in ((theirs, half), (mine, 0)):

        def rows(at, carry, out=out, base=base):
            here = pl.ds(pl.multiple_of(base + at * step, step), step)
            total = jnp.dot(block[here, :slab], before[...], preferred_element_type=F32)
            total += jnp.dot(block[here, slab : 2 * slab], own, preferred_element_type=F32)
            total += jnp.dot(block[here, 2 * slab :], after[...], preferred_element_type=F32)
            out[pl.ds(pl.multiple_of(at * step, step), step), :] = total.astype(BF16)
            return carry

        lax.fori_loop(0, half // step, rows, 0)


def aggregate(where, index, count, tiles, before, feats, after, scale, part_rows):
    slab, width = feats.shape
    flops = 2 * part_rows * 3 * slab * width
    return pl.pallas_call(
        aggregate_kernel,
        name="aggregate",
        out_shape=(
            jax.ShapeDtypeStruct((part_rows // 2, width), BF16),
            jax.ShapeDtypeStruct((part_rows // 2, width), BF16),
            jax.ShapeDtypeStruct((part_rows, slab), BF16),
        ),
        in_specs=smem(3) + vmem(5),
        out_specs=tuple(vmem(3)),
        scratch_shapes=[pltpu.VMEM((part_rows, 3 * slab), BF16)],
        compiler_params=pltpu.CompilerParams(vmem_limit_bytes=GRANT),
        cost_estimate=pl.CostEstimate(flops=flops, bytes_accessed=4 << 20, transcendentals=0),
    )(where, index, count, tiles, before, feats, after, scale)


def assemble_kernel(where, *refs):
    *blocks, out = refs
    cols = blocks[0].shape[1]
    for at, block in zip(origins(where[0], len(blocks) // CORES), blocks):
        out[:, pl.ds(pl.multiple_of(at * cols, cols), cols)] = block[...]


def assemble(where, blocks):
    depth, cols = blocks[0].shape
    width = cols * len(blocks)
    return pl.pallas_call(
        assemble_kernel,
        name="assemble",
        out_shape=jax.ShapeDtypeStruct((depth, width), BF16),
        in_specs=smem(1) + vmem(len(blocks)),
        out_specs=pl.BlockSpec(memory_space=pltpu.VMEM),
        compiler_params=pltpu.CompilerParams(vmem_limit_bytes=GRANT),
        cost_estimate=pl.CostEstimate(flops=0, bytes_accessed=4 << 20, transcendentals=0),
    )(where, *blocks)


def layer_kernel(mine, other, one, two, three, scale, weight, cot, out, grad, pieces):
    _, width = one.shape
    cols = pieces.shape[2]
    total = mine[...].astype(F32) + other[...].astype(F32)
    total += one[...].astype(F32) + two[...].astype(F32) + three[...].astype(F32)
    kept = total.astype(BF16)
    for at in range(width // cols):
        pieces[at] = kept[:, at * cols : (at + 1) * cols]
    scaled = (total * scale[...]).astype(BF16)
    step = 256
    for at in range(0, width, step):
        here = slice(at, at + step)
        pre = jnp.dot(scaled, weight[:, here], preferred_element_type=F32)
        sig = jax.nn.sigmoid(pre)
        out[:, here] = (pre * sig).astype(BF16)
        slope = sig * (1.0 + pre * (1.0 - sig))
        grad[:, here] = (cot[:, here].astype(F32) * slope * scale[...]).astype(BF16)


def layer(mine, other, arrived, scale, weight, cot):
    slab, width = cot.shape
    cols = TILE
    whole = lambda *shape: pl.BlockSpec(shape, lambda i: (0,) * len(shape))
    row = whole(slab, width)
    return pl.pallas_call(
        layer_kernel,
        name="layer",
        grid=(1,),
        out_shape=(
            jax.ShapeDtypeStruct((slab, width), BF16),
            jax.ShapeDtypeStruct((slab, width), BF16),
            jax.ShapeDtypeStruct((width // cols, slab, cols), BF16),
        ),
        in_specs=[row] * 5 + [whole(slab, 1), whole(width, width), row],
        out_specs=(row, row, whole(width // cols, slab, cols)),
        compiler_params=pltpu.CompilerParams(vmem_limit_bytes=GRANT),
        cost_estimate=pl.CostEstimate(
            flops=2 * slab * width * width, bytes_accessed=4 << 20, transcendentals=slab * width
        ),
    )(mine, other, *arrived, scale, weight, cot)


def term_kernel(where, aggs, *refs):
    *grads, out = refs
    blocks, _, rows, cols = out.shape
    total = None
    for at, grad in zip(origins(where[0], len(grads) // CORES), grads):
        part = lax.dot_general(
            aggs[at], grad[...], (((0,), (0,)), ((), ())), preferred_element_type=F32
        )
        total = part if total is None else total + part
    total = total.astype(BF16)
    for i in range(blocks):
        for j in range(out.shape[1]):
            out[i, j] = total[i * rows : (i + 1) * rows, j * cols : (j + 1) * cols]


def term(where, aggs, grads):
    _, slab, cols = aggs.shape
    width = grads[0].shape[1]
    return pl.pallas_call(
        term_kernel,
        name="term",
        out_shape=jax.ShapeDtypeStruct((RING, width // cols, cols // RING, cols), BF16),
        in_specs=smem(1) + vmem(1 + len(grads)),
        out_specs=pl.BlockSpec(memory_space=pltpu.VMEM),
        compiler_params=pltpu.CompilerParams(vmem_limit_bytes=GRANT),
        cost_estimate=pl.CostEstimate(
            flops=2 * slab * width * width, bytes_accessed=3 << 20, transcendentals=0
        ),
    )(where, aggs, *grads)


def sources_kernel(middle, weight, scale, *refs):
    *grads, out = refs
    slab = grads[0].shape[0]
    mixed = None
    for at, grad in enumerate(grads):
        part = lax.dot_general(
            middle[at * slab : (at + 1) * slab, :],
            grad[...],
            (((0,), (0,)), ((), ())),
            preferred_element_type=F32,
        )
        mixed = part if mixed is None else mixed + part
    back = lax.dot_general(
        mixed.astype(BF16), weight[...], (((1,), (1,)), ((), ())), preferred_element_type=F32
    )
    out[...] = (back * scale[...]).astype(BF16)


def source_grads(middle, weight, scale, grads):
    slab, width = grads[0].shape
    return pl.pallas_call(
        sources_kernel,
        name="source_grads",
        out_shape=jax.ShapeDtypeStruct((slab, width), BF16),
        in_specs=vmem(3 + len(grads)),
        out_specs=pl.BlockSpec(memory_space=pltpu.VMEM),
        compiler_params=pltpu.CompilerParams(vmem_limit_bytes=GRANT),
        cost_estimate=pl.CostEstimate(
            flops=4 * slab * width * width, bytes_accessed=5 << 20, transcendentals=0
        ),
    )(middle, weight, scale, *grads)


def per_device(features, history, degree, adj_tiles, tile_index, tile_count, weight, cotangent):
    slab, width = features.shape
    cols, rows = lax.axis_size("col"), lax.axis_size("row")
    chips = cols // CORES
    part_rows = slab * cols
    outer = rows // RING
    near = [[RING * i + j for j in range(RING)] for i in range(outer)]
    far = [[RING * i + j for i in range(outer)] for j in range(RING)]
    where = lax.axis_index("col").astype(jnp.int32)[None]
    scale = inverse_root(degree)[:, None]
    hist_src = (history.astype(F32) * scale).astype(BF16)
    before, after = neighbours(hist_src, "row")
    weights = gather(weight)
    mine, theirs, middle = aggregate(
        where, tile_index, tile_count, adj_tiles, before, features, after, scale, part_rows
    )
    other = swap(theirs)
    arrived = []
    for by in range(1, chips):
        here = slice(by * slab, (by + 1) * slab)
        pair = mine[here].astype(F32) + other[here].astype(F32)
        arrived.append(rotate(pair.astype(BF16), by))
    whole_weight = assemble(where, weights)
    layer_out, grad, pieces = layer(mine, other, arrived, scale, whole_weight, cotangent)
    grads = gather(grad)
    aggs = lax.all_to_all(pieces, "col", 0, 0, tiled=True)
    parts = term(where, aggs, grads)
    grad_features = source_grads(middle, whole_weight, scale, grads)

    def total(x):
        return jnp.sum(x.astype(F32), axis=0)

    def spread(x, groups):
        count = len(groups[0])
        every = jnp.broadcast_to(x[None], (count, *x.shape))
        return lax.all_to_all(every, "row", 0, 0, tiled=True, axis_index_groups=groups)

    summed = lax.all_to_all(parts, "row", 0, 0, tiled=True, axis_index_groups=near)
    owned = lax.all_to_all(total(summed).astype(BF16), "col", 0, 0, tiled=True)
    done = total(spread(owned, far)) * (1.0 / math.sqrt(part_rows * rows))
    every = spread(done.astype(BF16), near)
    grad_weight = every.astype(F32).transpose(1, 0, 2, 3).reshape(width, width // cols)
    return layer_out, grad_features, grad_weight


def solution(mesh):
    both = ("row", "col")
    in_specs = (
        P(both, None),
        P(both, None),
        P(both),
        P(both, None, None),
        P(both),
        P(both),
        P(None, "col"),
        P(both, None),
    )
    out_specs = (P(both, None), P(both, None), P(None, "col"))
    return jax.shard_map(
        per_device, mesh=mesh, in_specs=in_specs, out_specs=out_specs, check_vma=False
    )
```

```python
import math

import jax
import jax.numpy as jnp
from jax import lax
from jax.experimental import pallas as pl
from jax.experimental.pallas import tpu as pltpu
from jax.sharding import PartitionSpec as P

TILE = 128
CORES = 2
RING = 8
PAD = 16
GRANT = 12 << 20
F32 = jnp.float32
BF16 = jnp.bfloat16


def paired(x, axis, start):
    pairs = [(i, i + 1) for i in range(start, lax.axis_size(axis) - 1, 2)]
    return lax.ppermute(x, axis, pairs + [(j, i) for i, j in pairs])


def swap(x):
    return lax.ppermute(x, "col", [(i, i ^ 1) for i in range(lax.axis_size("col"))])


def rotate(x, by):
    cols = lax.axis_size("col")
    chips = cols // CORES
    pairs = [(i, (i // CORES + by) % chips * CORES + i % CORES) for i in range(cols)]
    return lax.ppermute(x, "col", pairs)


def gather(x):
    chips = lax.axis_size("col") // CORES
    same = [x] + [rotate(x, by) for by in range(1, chips)]
    return same + [swap(block) for block in same]


def origins(me, chips):
    chip, core = me // CORES, me % CORES
    same = [(chip - by + chips) % chips * CORES + core for by in range(chips)]
    return same + [at + 1 - 2 * core for at in same]


def vmem(count):
    return [pl.BlockSpec(memory_space=pltpu.VMEM)] * count


def smem(count):
    return [pl.BlockSpec(memory_space=pltpu.SMEM)] * count


def call(kernel, outs, ins, scratch=(), flops=0, transcendentals=0):
    specs = vmem(len(outs))
    return pl.pallas_call(
        kernel,
        out_shape=tuple(jax.ShapeDtypeStruct(shape, kind) for shape, kind in outs),
        in_specs=smem(ins[0]) + vmem(ins[1]),
        out_specs=tuple(specs),
        scratch_shapes=list(scratch),
        compiler_params=pltpu.CompilerParams(vmem_limit_bytes=GRANT),
        cost_estimate=pl.CostEstimate(
            flops=flops, bytes_accessed=2 << 20, transcendentals=transcendentals
        ),
    )


def pack_kernel(where, cot, weight, degree, out):
    count, _, cols = out.shape
    slab = cot.shape[0]
    depth = out.shape[1] - slab - PAD
    part = weight[pl.ds(pl.multiple_of(where[1] * depth, depth), depth), :]
    row = jnp.broadcast_to(degree[...].astype(F32).astype(BF16), (PAD, cols))
    for at in range(count):
        out[at, :slab, :] = cot[:, at * cols : (at + 1) * cols]
        out[at, slab : slab + depth, :] = part
        out[at, slab + depth :, :] = row


def prepare_kernel(where, index, count, tiles, feats, scale, block, middle, own):
    slots, slab = tiles.shape[0], feats.shape[0]
    width = 3 * slab // TILE
    part_rows = block.shape[0]
    chips = part_rows // slab // CORES
    chip, core = where[0] // CORES, where[0] % CORES
    block[...] = jnp.zeros_like(block)
    middle[...] = jnp.zeros_like(middle)
    for slot in range(slots):

        @pl.when(slot < count[0])
        def _():
            code = index[slot]
            dest, src = code // width, code % width
            other = (dest % CORES + core) % CORES * chips
            ahead = (dest // CORES - chip + chips) % chips
            row = pl.multiple_of((other + ahead) * TILE, TILE)
            odd = where[1] % 2
            col = pl.multiple_of((src + 2 * odd * (1 - src)) * TILE, TILE)
            block[pl.ds(row, TILE), pl.ds(col, TILE)] = tiles[slot]

            @pl.when(src == 1)
            def _():
                middle[pl.ds(pl.multiple_of(dest * TILE, TILE), TILE), :] = tiles[slot]

    own[...] = (feats[...].astype(F32) * scale[...]).astype(BF16)


def aggregate_kernel(block, first, own, second, mine, theirs):
    slab = own.shape[0]
    half = mine.shape[0]
    step = 256
    for out, base in ((theirs, half), (mine, 0)):
        for at in range(0, half, step):
            here = slice(base + at, base + at + step)
            total = jnp.dot(block[here, :slab], first[...], preferred_element_type=F32)
            total += jnp.dot(block[here, slab : 2 * slab], own[...], preferred_element_type=F32)
            total += jnp.dot(block[here, 2 * slab :], second[...], preferred_element_type=F32)
            out[at : at + step, :] = total.astype(BF16)


def main_kernel(where, packed, weight, *refs):
    *aggs, grads, parts = refs
    slab, width = aggs[0].shape
    pieces = parts.shape[0]
    rows = lax.broadcasted_iota(jnp.int32, (slab, slab), 0)
    eye = rows == lax.broadcasted_iota(jnp.int32, (slab, slab), 1)
    total = None
    for at, agg in zip(origins(where[0], len(aggs) // CORES), aggs):
        degree = packed[at, packed.shape[1] - PAD :, :][:1, :].astype(F32)
        scale = jnp.sum(jnp.where(eye, 1.0 / jnp.sqrt(degree), 0.0), axis=1, keepdims=True)
        pre = jnp.dot(agg[...], weight[...], preferred_element_type=F32) * scale
        sig = jax.nn.sigmoid(pre)
        slope = sig * (1.0 + pre * (1.0 - sig))
        grad = (packed[at, :slab, :].astype(F32) * slope * scale).astype(BF16)
        grads[pl.ds(pl.multiple_of(at * slab, slab), slab), :] = grad
        part = lax.dot_general(
            grad, agg[...], (((0,), (0,)), ((), ())), preferred_element_type=F32
        )
        total = part if total is None else total + part
    total = total.astype(BF16)
    for at in range(pieces):
        parts[at] = total[:, at * (width // pieces) : (at + 1) * (width // pieces)]


def final_kernel(where, weight, other, agg, middle, scale, *refs):
    *same, others, layer_out, out, mixed, whole = refs
    outer, chips, depth, cols = weight.shape
    for blocks, core in ((weight, where[0] % CORES), (other, 1 - where[0] % CORES)):
        for chip in range(chips):
            here = pl.ds(pl.multiple_of((chip * CORES + core) * cols, cols), cols)
            for step in range(outer):
                whole[step * depth : (step + 1) * depth, here] = blocks[step, chip]
    step = 256
    for at in range(0, out.shape[1], step):
        here = slice(at, at + step)
        pre = jnp.dot(agg[...], whole[:, here], preferred_element_type=F32) * scale[...]
        layer_out[:, here] = (pre * jax.nn.sigmoid(pre)).astype(BF16)
    grads = [*same, *[others.at[at] for at in range(chips)]]
    for at, grad in zip(origins(where[0], chips), grads):
        part = lax.dot_general(
            middle[...], grad[...], (((0,), (0,)), ((), ())), preferred_element_type=F32
        )
        mixed[:, pl.ds(pl.multiple_of(at * cols, cols), cols)] = part.astype(BF16)
    for at in range(0, out.shape[1], step):
        here = slice(at, at + step)
        back = lax.dot_general(
            mixed[...], whole[here, :], (((1,), (1,)), ((), ())), preferred_element_type=F32
        )
        out[:, here] = (back * scale[...]).astype(BF16)


def per_device(features, history, degree, adj_tiles, tile_index, tile_count, weight, cotangent):
    slab, width = features.shape
    cols, rows = lax.axis_size("col"), lax.axis_size("row")
    chips = cols // CORES
    part_rows = slab * cols
    out_cols = width // cols
    depth = width // RING
    outer = rows // RING
    near = [[RING * i + j for j in range(RING)] for i in range(outer)]
    half = rows // 2
    across = [
        [half * i + RING * k + j for k in range(outer // 2)] for i in range(2) for j in range(RING)
    ]
    where = jnp.stack([lax.axis_index("col"), lax.axis_index("row") % RING]).astype(jnp.int32)

    def total(x):
        return jnp.sum(x.astype(F32), axis=0)

    def over_row(x, groups):
        return lax.all_to_all(x, "row", 0, 0, tiled=True, axis_index_groups=groups)

    def replicated(x, groups):
        count = len(groups[0])
        return over_row(jnp.broadcast_to(x[None], (count, *x.shape)), groups)

    scale = (1.0 / jnp.sqrt(degree.astype(F32)))[:, None]
    hist_src = (history.astype(F32) * scale).astype(BF16)
    first = paired(hist_src, "row", 1)
    second = paired(hist_src, "row", 0)
    packed = call(
        pack_kernel, [((cols, slab + depth + PAD, out_cols), BF16)], (1, 3)
    )(where, cotangent, weight, degree[None])[0]
    packed = lax.all_to_all(packed, "col", 0, 0, tiled=True)
    block, middle, own = call(
        prepare_kernel,
        [((part_rows, 3 * slab), BF16), ((part_rows, slab), BF16), ((slab, width), BF16)],
        (3, 3),
    )(where, tile_index, tile_count, adj_tiles, features, scale)
    mine, theirs = call(
        aggregate_kernel,
        [((part_rows // CORES, width), BF16)] * 2,
        (0, 4),
        flops=6 * part_rows * slab * width,
    )(block, first, own, second)
    other = swap(theirs)
    arrived = []
    for by in range(1, chips):
        here = slice(by * slab, (by + 1) * slab)
        ahead = (mine[here].astype(F32) + other[here].astype(F32)).astype(BF16)
        arrived.append(rotate(ahead, by))
    agg = mine[:slab].astype(F32) + other[:slab].astype(F32)
    agg = (agg + sum(block.astype(F32) for block in arrived)).astype(BF16)
    core = where[0] % CORES
    mine_cols = packed.reshape(chips, CORES, slab + depth + PAD, out_cols)
    mine_cols = lax.dynamic_index_in_dim(mine_cols, core, 1, keepdims=False)
    half_weight = replicated(mine_cols[:, slab : slab + depth, :], near)
    other_weight = swap(half_weight)
    aggs = gather(agg)
    grad, parts = call(
        main_kernel,
        [((part_rows, out_cols), BF16), ((RING, out_cols, depth), BF16)],
        (1, 2 + cols),
        flops=4 * part_rows * width * out_cols,
        transcendentals=part_rows * out_cols,
    )(where, packed, weight, *aggs)
    summed = over_row(parts, near)
    grads = [grad] + [rotate(grad, by) for by in range(1, chips)]
    others = swap(jnp.stack(grads))
    summed = total(summed).T.astype(BF16)
    summed = replicated(summed, across)
    summed = total(summed).astype(BF16)
    opposite = lax.ppermute(summed, "row", [(i, (i + half) % rows) for i in range(rows)])
    summed = summed.astype(F32) + opposite.astype(F32)
    summed = summed * (1.0 / math.sqrt(part_rows * rows))
    summed = replicated(summed.astype(BF16), near)
    grad_weight = summed.reshape(width, out_cols).astype(F32)
    layer_out, grad_features = call(
        final_kernel,
        [((slab, width), BF16)] * 2,
        (1, 6 + chips),
        [pltpu.VMEM((slab, width), BF16), pltpu.VMEM((width, width), BF16)],
        flops=6 * slab * width * width,
        transcendentals=slab * width,
    )(where, half_weight, other_weight, agg, middle, scale, *grads, others)
    return layer_out, grad_features, grad_weight


def solution(mesh):
    both = ("row", "col")
    in_specs = (
        P(both, None),
        P(both, None),
        P(both),
        P(both, None, None),
        P(both),
        P(both),
        P(None, "col"),
        P(both, None),
    )
    out_specs = (P(both, None), P(both, None), P(None, "col"))
    return jax.shard_map(
        per_device, mesh=mesh, in_specs=in_specs, out_specs=out_specs, check_vma=False
    )
```

```python
import math

import jax
import jax.numpy as jnp
from jax import lax
from jax.experimental import pallas as pl
from jax.experimental.pallas import tpu as pltpu
from jax.sharding import PartitionSpec as P

TILE = 128
CORES = 2
RING = 8
PAD = 16
GRANT = 12 << 20
F32 = jnp.float32
BF16 = jnp.bfloat16


def paired(x, axis, start):
    pairs = [(i, i + 1) for i in range(start, lax.axis_size(axis) - 1, 2)]
    return lax.ppermute(x, axis, pairs + [(j, i) for i, j in pairs])


def swap(x):
    return lax.ppermute(x, "col", [(i, i ^ 1) for i in range(lax.axis_size("col"))])


def rotate(x, by):
    cols = lax.axis_size("col")
    chips = cols // CORES
    pairs = [(i, (i // CORES + by) % chips * CORES + i % CORES) for i in range(cols)]
    return lax.ppermute(x, "col", pairs)


def gather(x):
    chips = lax.axis_size("col") // CORES
    same = [x] + [rotate(x, by) for by in range(1, chips)]
    swapped = []
    for block in same:
        swapped.append(swap(block))
    return same + swapped


def origins(me, chips):
    chip, core = me // CORES, me % CORES
    same = [(chip - by + chips) % chips * CORES + core for by in range(chips)]
    return same + [at + 1 - 2 * core for at in same]


def vmem(count):
    return [pl.BlockSpec(memory_space=pltpu.VMEM)] * count


def smem(count):
    return [pl.BlockSpec(memory_space=pltpu.SMEM)] * count


def call(kernel, outs, ins, scratch=(), flops=0, transcendentals=0):
    specs = vmem(len(outs))
    return pl.pallas_call(
        kernel,
        out_shape=tuple(jax.ShapeDtypeStruct(shape, kind) for shape, kind in outs),
        in_specs=smem(ins[0]) + vmem(ins[1]),
        out_specs=tuple(specs),
        scratch_shapes=list(scratch),
        compiler_params=pltpu.CompilerParams(vmem_limit_bytes=GRANT),
        cost_estimate=pl.CostEstimate(
            flops=flops, bytes_accessed=2 << 20, transcendentals=transcendentals
        ),
    )


def pack_kernel(where, cot, weight, degree, out):
    count, _, cols = out.shape
    slab = cot.shape[0]
    depth = out.shape[1] - slab - PAD
    part = weight[pl.ds(pl.multiple_of(where[1] * depth, depth), depth), :]
    row = jnp.broadcast_to(degree[...].astype(F32).astype(BF16), (PAD, cols))
    for at in range(count):
        out[at, :slab, :] = cot[:, at * cols : (at + 1) * cols]
        out[at, slab : slab + depth, :] = part
        out[at, slab + depth :, :] = row


def prepare_kernel(where, index, count, tiles, feats, scale, block, middle, own):
    slots, slab = tiles.shape[0], feats.shape[0]
    width = 3 * slab // TILE
    part_rows = block.shape[0]
    chips = part_rows // slab // CORES
    chip, core = where[0] // CORES, where[0] % CORES
    block[...] = jnp.zeros_like(block)
    middle[...] = jnp.zeros_like(middle)
    for slot in range(slots):

        @pl.when(slot < count[0])
        def _():
            code = index[slot]
            dest, src = code // width, code % width
            other = (dest % CORES + core) % CORES * chips
            ahead = (dest // CORES - chip + chips) % chips
            row = pl.multiple_of((other + ahead) * TILE, TILE)
            odd = where[1] % 2
            col = pl.multiple_of((src + 2 * odd * (1 - src)) * TILE, TILE)
            block[pl.ds(row, TILE), pl.ds(col, TILE)] = tiles[slot]

            @pl.when(src == 1)
            def _():
                middle[pl.ds(pl.multiple_of(dest * TILE, TILE), TILE), :] = tiles[slot]

    own[...] = (feats[...].astype(F32) * scale[...]).astype(BF16)


def aggregate_kernel(block, first, own, second, mine, theirs):
    slab = own.shape[0]
    half = mine.shape[0]
    step = 256
    for out, base in ((theirs, half), (mine, 0)):
        for at in range(0, half, step):
            here = slice(base + at, base + at + step)
            total = jnp.dot(block[here, :slab], first[...], preferred_element_type=F32)
            total += jnp.dot(block[here, slab : 2 * slab], own[...], preferred_element_type=F32)
            total += jnp.dot(block[here, 2 * slab :], second[...], preferred_element_type=F32)
            out[at : at + step, :] = total.astype(BF16)


def pair_kernel(mine, other, kept, *ahead):
    slab = kept.shape[0]
    kept[...] = mine[:slab, :].astype(F32) + other[:slab, :].astype(F32)
    for at, out in enumerate(ahead, 1):
        here = slice(at * slab, (at + 1) * slab)
        out[...] = (mine[here, :].astype(F32) + other[here, :].astype(F32)).astype(BF16)


def main_kernel(where, packed, weight, *refs):
    *aggs, grads, parts, other_scale = refs
    slab, width = aggs[0].shape
    pieces = parts.shape[0]
    rows = lax.broadcasted_iota(jnp.int32, (slab, slab), 0)
    eye = rows == lax.broadcasted_iota(jnp.int32, (slab, slab), 1)
    total = None
    chips = len(aggs) // CORES
    for place, (at, agg) in enumerate(zip(origins(where[0], chips), aggs)):
        degree = packed[at, packed.shape[1] - PAD :, :][:1, :].astype(F32)
        scale = jnp.sum(jnp.where(eye, 1.0 / jnp.sqrt(degree), 0.0), axis=1, keepdims=True)
        if place == chips:
            other_scale[...] = scale
        pre = jnp.dot(agg[...], weight[...], preferred_element_type=F32) * scale
        sig = jax.nn.sigmoid(pre)
        slope = sig * (1.0 + pre * (1.0 - sig))
        grad = (packed[at, :slab, :].astype(F32) * slope * scale).astype(BF16)
        grads[pl.ds(pl.multiple_of(at * slab, slab), slab), :] = grad
        part = lax.dot_general(
            grad, agg[...], (((0,), (0,)), ((), ())), preferred_element_type=F32
        )
        total = part if total is None else total + part
    total = total.astype(BF16)
    for at in range(pieces):
        parts[at] = total[:, at * (width // pieces) : (at + 1) * (width // pieces)]


def final_kernel(where, weight, agg, other_agg, middle, other_middle, scale, other_scale, *refs):
    *grads, lines, out, theirs, mixed, whole = refs
    outer, chips, depth, cols = weight.shape
    slab, width = out.shape
    for at in range(chips):
        for step in range(outer):
            here = slice(step * depth, (step + 1) * depth)
            whole[here, at * cols : (at + 1) * cols] = weight[step, at]
    for rows, factor, target, base in (
        (agg, scale, lines, 0),
        (other_agg, other_scale, theirs, width),
    ):
        pre = jnp.dot(rows[...], whole[...], preferred_element_type=F32) * factor[...]
        target[:, base : base + chips * cols] = (pre * jax.nn.sigmoid(pre)).astype(BF16)
    chip = where[0] // CORES
    for by, grad in enumerate(grads):
        at = (chip - by + chips) % chips
        here = pl.ds(pl.multiple_of(at * cols, cols), cols)
        for place, block in enumerate((middle, other_middle)):
            part = lax.dot_general(
                block[...], grad[...], (((0,), (0,)), ((), ())), preferred_element_type=F32
            )
            mixed[place * slab : (place + 1) * slab, here] = part.astype(BF16)
    step = 256
    for at in range(0, width, step):
        here = slice(at, at + step)
        back = lax.dot_general(
            mixed[...], whole[here, :], (((1,), (1,)), ((), ())), preferred_element_type=F32
        )
        out[:, here] = back[:slab]
        theirs[:, here] = back[slab:].astype(BF16)


def finish_kernel(where, lines, back, arrived, scale, layer_out, out):
    _, width = out.shape
    core = where[0] % CORES
    cols = TILE
    out[...] = ((back[...] + arrived[:, :width].astype(F32)) * scale[...]).astype(BF16)
    for at in range(lines.shape[1] // cols):
        here = slice(at * cols, (at + 1) * cols)
        mine = pl.ds(pl.multiple_of((at * CORES + core) * cols, cols), cols)
        other = pl.ds(pl.multiple_of((at * CORES + 1 - core) * cols, cols), cols)
        layer_out[:, mine] = lines[:, here]
        layer_out[:, other] = arrived[:, width + at * cols : width + (at + 1) * cols]


def per_device(features, history, degree, adj_tiles, tile_index, tile_count, weight, cotangent):
    slab, width = features.shape
    cols, rows = lax.axis_size("col"), lax.axis_size("row")
    chips = cols // CORES
    part_rows = slab * cols
    out_cols = width // cols
    depth = width // RING
    outer = rows // RING
    near = [[RING * i + j for j in range(RING)] for i in range(outer)]
    half = rows // 2
    across = [
        [half * i + RING * k + j for k in range(outer // 2)] for i in range(2) for j in range(RING)
    ]
    where = jnp.stack([lax.axis_index("col"), lax.axis_index("row") % RING]).astype(jnp.int32)

    def total(x):
        return jnp.sum(x.astype(F32), axis=0)

    def over_row(x, groups):
        return lax.all_to_all(x, "row", 0, 0, tiled=True, axis_index_groups=groups)

    def replicated(x, groups):
        count = len(groups[0])
        return over_row(jnp.broadcast_to(x[None], (count, *x.shape)), groups)

    scale = (1.0 / jnp.sqrt(degree.astype(F32)))[:, None]
    hist_src = (history.astype(F32) * scale).astype(BF16)
    first = paired(hist_src, "row", 1)
    second = paired(hist_src, "row", 0)
    packed = call(
        pack_kernel, [((cols, slab + depth + PAD, out_cols), BF16)], (1, 3)
    )(where, cotangent, weight, degree[None])[0]
    packed = lax.all_to_all(packed, "col", 0, 0, tiled=True)
    block, middle, own = call(
        prepare_kernel,
        [((part_rows, 3 * slab), BF16), ((part_rows, slab), BF16), ((slab, width), BF16)],
        (3, 3),
    )(where, tile_index, tile_count, adj_tiles, features, scale)
    mine, theirs = call(
        aggregate_kernel,
        [((part_rows // CORES, width), BF16)] * 2,
        (0, 4),
        flops=6 * part_rows * slab * width,
    )(block, first, own, second)
    other = swap(theirs)
    kept, *ahead = call(
        pair_kernel, [((slab, width), F32)] + [((slab, width), BF16)] * (chips - 1), (0, 2)
    )(mine, other)
    arrived = [rotate(block, by) for by, block in enumerate(ahead, 1)]
    agg = (kept + sum(block.astype(F32) for block in arrived)).astype(BF16)
    core = where[0] % CORES
    mine_cols = packed.reshape(chips, CORES, slab + depth + PAD, out_cols)
    mine_cols = lax.dynamic_index_in_dim(mine_cols, core, 1, keepdims=False)
    half_weight = replicated(mine_cols[:, slab : slab + depth, :], near)
    other_middle = swap(middle)
    aggs = gather(agg)
    grad, parts, other_scale = call(
        main_kernel,
        [
            ((part_rows, out_cols), BF16),
            ((RING, out_cols, depth), BF16),
            ((slab, 1), F32),
        ],
        (1, 2 + cols),
        flops=4 * part_rows * width * out_cols,
        transcendentals=part_rows * out_cols,
    )(where, packed, weight, *aggs)
    summed = over_row(parts, near)
    grads = [grad]
    for by in range(1, chips):
        grads.append(rotate(grad, by))
    summed = total(summed).T.astype(BF16)
    summed = replicated(summed, across)
    summed = total(summed).astype(BF16)
    opposite = lax.ppermute(summed, "row", [(i, (i + half) % rows) for i in range(rows)])
    summed = summed.astype(F32) + opposite.astype(F32)
    summed = summed * (1.0 / math.sqrt(part_rows * rows))
    summed = replicated(summed.astype(BF16), near)
    grad_weight = summed.reshape(width, out_cols).astype(F32)
    own_cols = chips * out_cols
    lines, back, theirs = call(
        final_kernel,
        [((slab, own_cols), BF16), ((slab, width), F32), ((slab, width + own_cols), BF16)],
        (1, 7 + chips),
        [pltpu.VMEM((CORES * slab, own_cols), BF16), pltpu.VMEM((width, own_cols), BF16)],
        flops=6 * slab * width * width,
        transcendentals=slab * width,
    )(where, half_weight, agg, aggs[chips], middle, other_middle, scale, other_scale, *grads)
    arrived = swap(theirs)
    layer_out, grad_features = call(
        finish_kernel, [((slab, width), BF16)] * 2, (1, 4)
    )(where, lines, back, arrived, scale)
    return layer_out, grad_features, grad_weight


def solution(mesh):
    both = ("row", "col")
    in_specs = (
        P(both, None),
        P(both, None),
        P(both),
        P(both, None, None),
        P(both),
        P(both),
        P(None, "col"),
        P(both, None),
    )
    out_specs = (P(both, None), P(both, None), P(None, "col"))
    return jax.shard_map(
        per_device, mesh=mesh, in_specs=in_specs, out_specs=out_specs, check_vma=False
    )
```

```python
import math

import jax
import jax.numpy as jnp
from jax import lax
from jax.experimental import pallas as pl
from jax.experimental.pallas import tpu as pltpu
from jax.sharding import PartitionSpec as P

TILE = 128
CORES = 2
RING = 8
PAD = 16
GRANT = 12 << 20
F32 = jnp.float32
BF16 = jnp.bfloat16


def paired(x, axis, start):
    pairs = [(i, i + 1) for i in range(start, lax.axis_size(axis) - 1, 2)]
    return lax.ppermute(x, axis, pairs + [(j, i) for i, j in pairs])


def swap(x):
    return lax.ppermute(x, "col", [(i, i ^ 1) for i in range(lax.axis_size("col"))])


def rotate(x, by):
    cols = lax.axis_size("col")
    chips = cols // CORES
    pairs = [(i, (i // CORES + by) % chips * CORES + i % CORES) for i in range(cols)]
    return lax.ppermute(x, "col", pairs)


def gather(x):
    chips = lax.axis_size("col") // CORES
    same = [x] + [rotate(x, by) for by in range(1, chips)]
    swapped = []
    for block in same:
        swapped.append(swap(block))
    return same + swapped


def origins(me, chips):
    chip, core = me // CORES, me % CORES
    same = [(chip - by + chips) % chips * CORES + core for by in range(chips)]
    return same + [at + 1 - 2 * core for at in same]


def vmem(count):
    return [pl.BlockSpec(memory_space=pltpu.VMEM)] * count


def smem(count):
    return [pl.BlockSpec(memory_space=pltpu.SMEM)] * count


def call(kernel, outs, ins, scratch=(), flops=0, transcendentals=0):
    specs = vmem(len(outs))
    return pl.pallas_call(
        kernel,
        out_shape=tuple(jax.ShapeDtypeStruct(shape, kind) for shape, kind in outs),
        in_specs=smem(ins[0]) + vmem(ins[1]),
        out_specs=tuple(specs),
        scratch_shapes=list(scratch),
        compiler_params=pltpu.CompilerParams(vmem_limit_bytes=GRANT),
        cost_estimate=pl.CostEstimate(
            flops=flops, bytes_accessed=2 << 20, transcendentals=transcendentals
        ),
    )


def pack_kernel(where, cot, weight, degree, out):
    count, _, cols = out.shape
    slab = cot.shape[0]
    depth = out.shape[1] - slab - PAD
    part = weight[pl.ds(pl.multiple_of(where[1] * depth, depth), depth), :]
    row = jnp.broadcast_to(degree[...].astype(F32).astype(BF16), (PAD, cols))
    for at in range(count):
        out[at, :slab, :] = cot[:, at * cols : (at + 1) * cols]
        out[at, slab : slab + depth, :] = part
        out[at, slab + depth :, :] = row


def prepare_kernel(where, index, count, tiles, feats, scale, block, middle, own):
    slots, slab = tiles.shape[0], feats.shape[0]
    width = 3 * slab // TILE
    part_rows = block.shape[0]
    chips = part_rows // slab // CORES
    chip, core = where[0] // CORES, where[0] % CORES
    block[...] = jnp.zeros_like(block)
    middle[...] = jnp.zeros_like(middle)
    for slot in range(slots):

        @pl.when(slot < count[0])
        def _():
            code = index[slot]
            dest, src = code // width, code % width
            other = (dest % CORES + core) % CORES * chips
            ahead = (dest // CORES - chip + chips) % chips
            row = pl.multiple_of((other + ahead) * TILE, TILE)
            odd = where[1] % 2
            col = pl.multiple_of((src + 2 * odd * (1 - src)) * TILE, TILE)
            block[pl.ds(row, TILE), pl.ds(col, TILE)] = tiles[slot]

            @pl.when(src == 1)
            def _():
                middle[pl.ds(pl.multiple_of(dest * TILE, TILE), TILE), :] = tiles[slot]

    own[...] = (feats[...].astype(F32) * scale[...]).astype(BF16)


def aggregate_kernel(block, first, own, second, mine, theirs):
    slab = own.shape[0]
    half = mine.shape[0]
    step = 256
    for out, base in ((theirs, half), (mine, 0)):
        for at in range(0, half, step):
            here = slice(base + at, base + at + step)
            total = jnp.dot(block[here, :slab], first[...], preferred_element_type=F32)
            total += jnp.dot(block[here, slab : 2 * slab], own[...], preferred_element_type=F32)
            total += jnp.dot(block[here, 2 * slab :], second[...], preferred_element_type=F32)
            out[at : at + step, :] = total.astype(BF16)


def pair_kernel(mine, other, kept, *ahead):
    slab = kept.shape[0]
    for at, out in enumerate((kept, *ahead)):
        here = slice(at * slab, (at + 1) * slab)
        out[...] = (mine[here, :].astype(F32) + other[here, :].astype(F32)).astype(BF16)


def main_kernel(where, packed, weight, *refs):
    *aggs, grads, parts, other_scale = refs
    slab, width = aggs[0].shape
    pieces = parts.shape[0]
    rows = lax.broadcasted_iota(jnp.int32, (slab, slab), 0)
    eye = rows == lax.broadcasted_iota(jnp.int32, (slab, slab), 1)
    total = None
    chips = len(aggs) // CORES
    for place, (at, agg) in enumerate(zip(origins(where[0], chips), aggs)):
        degree = packed[at, packed.shape[1] - PAD :, :][:1, :].astype(F32)
        scale = jnp.sum(jnp.where(eye, 1.0 / jnp.sqrt(degree), 0.0), axis=1, keepdims=True)
        if place == chips:
            other_scale[...] = scale
        pre = jnp.dot(agg[...], weight[...], preferred_element_type=F32) * scale
        sig = jax.nn.sigmoid(pre)
        slope = sig * (1.0 + pre * (1.0 - sig))
        grad = (packed[at, :slab, :].astype(F32) * slope * scale).astype(BF16)
        grads[pl.ds(pl.multiple_of(at * slab, slab), slab), :] = grad
        part = lax.dot_general(
            grad, agg[...], (((0,), (0,)), ((), ())), preferred_element_type=F32
        )
        total = part if total is None else total + part
    total = total.astype(BF16)
    for at in range(pieces):
        parts[at] = total[:, at * (width // pieces) : (at + 1) * (width // pieces)]


def final_kernel(where, weight, agg, other_agg, middle, other_middle, scale, other_scale, *refs):
    *grads, lines, out, theirs, mixed, whole = refs
    outer, chips, depth, cols = weight.shape
    slab, width = out.shape
    for at in range(chips):
        for step in range(outer):
            here = slice(step * depth, (step + 1) * depth)
            whole[here, at * cols : (at + 1) * cols] = weight[step, at]
    for rows, factor, target, base in (
        (agg, scale, lines, 0),
        (other_agg, other_scale, theirs, width),
    ):
        pre = jnp.dot(rows[...], whole[...], preferred_element_type=F32) * factor[...]
        target[:, base : base + chips * cols] = (pre * jax.nn.sigmoid(pre)).astype(BF16)
    chip = where[0] // CORES
    for by, grad in enumerate(grads):
        at = (chip - by + chips) % chips
        here = pl.ds(pl.multiple_of(at * cols, cols), cols)
        for place, block in enumerate((middle, other_middle)):
            part = lax.dot_general(
                block[...], grad[...], (((0,), (0,)), ((), ())), preferred_element_type=F32
            )
            mixed[place * slab : (place + 1) * slab, here] = part.astype(BF16)
    step = 256
    for at in range(0, width, step):
        here = slice(at, at + step)
        back = lax.dot_general(
            mixed[...], whole[here, :], (((1,), (1,)), ((), ())), preferred_element_type=F32
        )
        out[:, here] = back[:slab]
        theirs[:, here] = back[slab:].astype(BF16)


def finish_kernel(where, lines, back, arrived, scale, layer_out, out):
    _, width = out.shape
    core = where[0] % CORES
    cols = TILE
    out[...] = ((back[...] + arrived[:, :width].astype(F32)) * scale[...]).astype(BF16)
    for at in range(lines.shape[1] // cols):
        here = slice(at * cols, (at + 1) * cols)
        mine = pl.ds(pl.multiple_of((at * CORES + core) * cols, cols), cols)
        other = pl.ds(pl.multiple_of((at * CORES + 1 - core) * cols, cols), cols)
        layer_out[:, mine] = lines[:, here]
        layer_out[:, other] = arrived[:, width + at * cols : width + (at + 1) * cols]


def per_device(features, history, degree, adj_tiles, tile_index, tile_count, weight, cotangent):
    slab, width = features.shape
    cols, rows = lax.axis_size("col"), lax.axis_size("row")
    chips = cols // CORES
    part_rows = slab * cols
    out_cols = width // cols
    depth = width // RING
    outer = rows // RING
    near = [[RING * i + j for j in range(RING)] for i in range(outer)]
    half = rows // 2
    across = [
        [half * i + RING * k + j for k in range(outer // 2)] for i in range(2) for j in range(RING)
    ]
    where = jnp.stack([lax.axis_index("col"), lax.axis_index("row") % RING]).astype(jnp.int32)

    def total(x):
        return jnp.sum(x.astype(F32), axis=0)

    def over_row(x, groups):
        return lax.all_to_all(x, "row", 0, 0, tiled=True, axis_index_groups=groups)

    def replicated(x, groups):
        count = len(groups[0])
        return over_row(jnp.broadcast_to(x[None], (count, *x.shape)), groups)

    scale = (1.0 / jnp.sqrt(degree.astype(F32)))[:, None]
    hist_src = (history.astype(F32) * scale).astype(BF16)
    first = paired(hist_src, "row", 1)
    second = paired(hist_src, "row", 0)
    packed = call(
        pack_kernel, [((cols, slab + depth + PAD, out_cols), BF16)], (1, 3)
    )(where, cotangent, weight, degree[None])[0]
    packed = lax.all_to_all(packed, "col", 0, 0, tiled=True)
    block, middle, own = call(
        prepare_kernel,
        [((part_rows, 3 * slab), BF16), ((part_rows, slab), BF16), ((slab, width), BF16)],
        (3, 3),
    )(where, tile_index, tile_count, adj_tiles, features, scale)
    mine, theirs = call(
        aggregate_kernel,
        [((part_rows // CORES, width), BF16)] * 2,
        (0, 4),
        flops=6 * part_rows * slab * width,
    )(block, first, own, second)
    other = swap(theirs)
    kept, *ahead = call(pair_kernel, [((slab, width), BF16)] * chips, (0, 2))(mine, other)
    arrived = [rotate(block, by) for by, block in enumerate(ahead, 1)]
    agg = sum(block.astype(F32) for block in (kept, *arrived)).astype(BF16)
    core = where[0] % CORES
    mine_cols = packed.reshape(chips, CORES, slab + depth + PAD, out_cols)
    mine_cols = lax.dynamic_index_in_dim(mine_cols, core, 1, keepdims=False)
    half_weight = replicated(mine_cols[:, slab : slab + depth, :], near)
    other_middle = swap(middle)
    aggs = gather(agg)
    grad, parts, other_scale = call(
        main_kernel,
        [
            ((part_rows, out_cols), BF16),
            ((RING, out_cols, depth), BF16),
            ((slab, 1), F32),
        ],
        (1, 2 + cols),
        flops=4 * part_rows * width * out_cols,
        transcendentals=part_rows * out_cols,
    )(where, packed, weight, *aggs)
    summed = over_row(parts, near)
    grads = [grad]
    for by in range(1, chips):
        grads.append(rotate(grad, by))
    summed = total(summed).T.astype(BF16)
    summed = replicated(summed, across)
    summed = total(summed).astype(BF16)
    opposite = lax.ppermute(summed, "row", [(i, (i + half) % rows) for i in range(rows)])
    summed = summed.astype(F32) + opposite.astype(F32)
    summed = summed * (1.0 / math.sqrt(part_rows * rows))
    summed = replicated(summed.astype(BF16), near)
    grad_weight = summed.reshape(width, out_cols).astype(F32)
    own_cols = chips * out_cols
    lines, back, theirs = call(
        final_kernel,
        [((slab, own_cols), BF16), ((slab, width), F32), ((slab, width + own_cols), BF16)],
        (1, 7 + chips),
        [pltpu.VMEM((CORES * slab, own_cols), BF16), pltpu.VMEM((width, own_cols), BF16)],
        flops=6 * slab * width * width,
        transcendentals=slab * width,
    )(where, half_weight, agg, aggs[chips], middle, other_middle, scale, other_scale, *grads)
    arrived = swap(theirs)
    layer_out, grad_features = call(
        finish_kernel, [((slab, width), BF16)] * 2, (1, 4)
    )(where, lines, back, arrived, scale)
    return layer_out, grad_features, grad_weight


def solution(mesh):
    both = ("row", "col")
    in_specs = (
        P(both, None),
        P(both, None),
        P(both),
        P(both, None, None),
        P(both),
        P(both),
        P(None, "col"),
        P(both, None),
    )
    out_specs = (P(both, None), P(both, None), P(None, "col"))
    return jax.shard_map(
        per_device, mesh=mesh, in_specs=in_specs, out_specs=out_specs, check_vma=False
    )
```
